128 devices in a mesh: dp: 16 (over y, z), ctx: 8 (over x, core).
Axes of the slice: x: 4, y: 4, z: 4, core: 2. Of those that a mesh axis runs over, the one named last changes fastest.
Arguments:
- query_rows: bfloat16 [32768, 8192], P(('dp', 'ctx')), may hold values from -34 to 34
- key_rows: bfloat16 [32768, 1024], P(('dp', 'ctx')), may hold values from -10 to 10, as said below
- value_rows: bfloat16 [32768, 1024], P(('dp', 'ctx')), may hold values from -6 to 6
- grad_out: bfloat16 [32768, 8192], P(('dp', 'ctx')), may hold values from -6 to 6
- dest_rows: int32 [32768], P(('dp', 'ctx')), may hold values from 0 to 32767, as said below
- key_blocks: int32 [16, 16, 4], P('dp', 'ctx'), may hold values from 0 to 15, as said below
- key_count: int32 [16, 16], P('dp', 'ctx'), may hold values from 1 to 4, as said below
Outputs:
- attn_out: bfloat16 [32768, 8192], P(('dp', 'ctx'))
- grad_query: bfloat16 [32768, 8192], P(('dp', 'ctx'))
- grad_key: bfloat16 [32768, 1024], P(('dp', 'ctx'))
- grad_value: bfloat16 [32768, 1024], P(('dp', 'ctx'))
The draws below stay inside these ranges and needn't reach their ends.
Inputs may be any that keep to these rules, and one draw needn't show every extreme that they name: `dest_rows`: A permutation of the learner rows; the 256 engine rows of each device hold exactly 2 rows for each device's 256 learner rows. `key_blocks`: each packed sequence is a run of token trees: a prompt of one or two blocks followed by two to four responses of one or two blocks each, the last tree possibly cut; the first tree has a prompt of two blocks and a first response of two blocks. For query block b the used entries, in increasing order, are the prompt blocks of b's tree and the blocks of b's own branch up to b itself; unused entries equal b. `key_count`: each packed sequence has a block that attends to 4 blocks. `key_rows`: keys of all heads.
All inputs are finite; a program needn't handle non-finite values.
Results may differ from the reference program's by a relative error of at most 0.02.
Values may be sent and summed in bfloat16 or wider, within the bound.
No kernel may reach another device: no remote copies, remote signals or barrier semaphores. Data moves between devices by JAX's collectives and lax.ppermute only.
A program may use at most 192 MiB of HBM per device.

```python
import jax
import jax.numpy as jnp
from jax import lax

QH = 64
KVH = 8
HD = 128
BLK = 128
KL = 4
TOK_DEV = 256
SEQ = 2048
NB = 16
TOKENS = 32768
CAP = 2
N_DP = 16
N_CTX = 8


def draw_query_rows(key, part):
    noise_part = jnp.clip(jax.random.normal(jax.random.fold_in(key, 1), (TOKENS, QH * HD), jnp.float32), -4.0, 4.0)
    values_out = noise_part
    return values_out.astype(jnp.bfloat16)


def draw_key_rows(key, part):
    noise_part = jnp.clip(jax.random.normal(jax.random.fold_in(key, 4), (TOKENS, KVH * HD), jnp.float32), -4.0, 4.0)
    values_out = noise_part
    return values_out.astype(jnp.bfloat16)


def draw_dest_rows(key, part):
    devices_all = N_DP * N_CTX
    learner_perm = jax.vmap(lambda sub_key: jax.random.permutation(sub_key, TOK_DEV))(jax.random.split(jax.random.fold_in(key, 21), devices_all)).astype(jnp.int32)
    by_sender = learner_perm.reshape(devices_all, devices_all, CAP)
    offsets = (jnp.arange(devices_all, dtype=jnp.int32) * TOK_DEV)[:, None, None]
    by_sender = jnp.transpose(by_sender + offsets, (1, 0, 2)).reshape(devices_all, TOK_DEV)
    sender_perm = jax.vmap(lambda sub_key: jax.random.permutation(sub_key, TOK_DEV))(jax.random.split(jax.random.fold_in(key, 22), devices_all)).astype(jnp.int32)
    rows_index = jnp.arange(devices_all, dtype=jnp.int32)[:, None]
    placed = jnp.zeros((devices_all, TOK_DEV), jnp.int32).at[rows_index, sender_perm].set(by_sender)
    return placed.reshape(TOKENS)


def tree_one(sub_key):
    coins = jax.random.randint(sub_key, (NB, 3), 0, 6).astype(jnp.int32)
    slot_range = jnp.arange(KL, dtype=jnp.int32)

    def advance(carry, inputs):
        prompt_first, prompt_last, resp_first, left_over, kind_now, resp_left = carry
        block_index, coin_row = inputs
        prompt_len = jnp.where(block_index == 0, 2, 1 + coin_row[0] % 2)
        resp_draw = 1 + coin_row[1] % 2
        tree_width = 2 + coin_row[2] % 3
        is_new = left_over == 0
        after_prompt = is_new & (kind_now == 0)
        next_resp = is_new & (kind_now == 1) & (resp_left > 0)
        new_prompt = is_new & (kind_now == 1) & (resp_left == 0)
        resp_len = jnp.where((prompt_first == 0) & after_prompt, 2, resp_draw)
        prompt_first = jnp.where(new_prompt, block_index, prompt_first)
        prompt_last = jnp.where(after_prompt, block_index - 1, prompt_last)
        resp_first = jnp.where(after_prompt | next_resp, block_index, resp_first)
        kind_next = jnp.where(new_prompt, 0, jnp.where(is_new, 1, kind_now))
        left_next = jnp.where(new_prompt, prompt_len - 1, jnp.where(is_new, resp_len - 1, left_over - 1))
        resp_next = jnp.where(new_prompt, tree_width, jnp.where(after_prompt | next_resp, resp_left - 1, resp_left))
        prompt_count = jnp.where(kind_next == 0, 0, prompt_last - prompt_first + 1)
        branch_first = jnp.where(kind_next == 0, prompt_first, resp_first)
        list_count = prompt_count + block_index - branch_first + 1
        entries = jnp.where(slot_range < prompt_count, prompt_first + slot_range, branch_first + slot_range - prompt_count)
        entries = jnp.where(slot_range < list_count, entries, block_index)
        carry_next = (prompt_first, prompt_last, resp_first, left_next, kind_next, resp_next)
        return (carry_next, (entries.astype(jnp.int32), list_count.astype(jnp.int32)))
    start = (jnp.int32(0), jnp.int32(0), jnp.int32(0), jnp.int32(0), jnp.int32(1), jnp.int32(0))
    ignored, outputs = lax.scan(advance, start, (jnp.arange(NB, dtype=jnp.int32), coins))
    return outputs


def tree_lists(key):
    return jax.vmap(tree_one)(jax.random.split(jax.random.fold_in(key, 11), N_DP))


def draw_key_blocks(key, part):
    return tree_lists(key)[0]


def draw_key_count(key, part):
    return tree_lists(key)[1]


def block_levels(stream_key, extent, cuts, least, high):
    loudness, own = 1.0, jax.random.fold_in(stream_key, 6)
    for position, shards_of in cuts:
        steps = jnp.exp(jax.random.uniform(jax.random.fold_in(own, position), (shards_of,), jnp.float32, least / len(cuts), high / len(cuts)))
        loudness = loudness * jnp.repeat(steps, extent[position] // shards_of).reshape([-1 if axis == position else 1 for axis in range(len(extent))])
    return loudness


def noise(key, extent, deviation, limit, cuts=(), held_as=jnp.bfloat16):
    gain = block_levels(key, extent, cuts, -0.22, 0.18) if cuts else 1.0
    values = jax.random.normal(key, extent, jnp.float32) * deviation * gain
    return jnp.minimum(jnp.maximum(values, -limit), limit).astype(held_as)


def setup_inputs(seed: int = 0) -> dict:
    streams_of = jax.random.split(jax.random.key(seed), 8)
    query_rows = draw_query_rows(jax.random.fold_in(streams_of[7], 71), 0)
    key_rows = draw_key_rows(jax.random.fold_in(streams_of[7], 71), 0)
    value_rows = noise(streams_of[2], (TOKENS, KVH * HD), 1.0, 6.0, ((0, 128),))
    grad_out = noise(streams_of[3], (TOKENS, QH * HD), 1.0, 6.0, ((0, 128),))
    dest_rows = draw_dest_rows(jax.random.fold_in(streams_of[7], 71), 0)
    key_blocks = draw_key_blocks(jax.random.fold_in(streams_of[7], 71), 0)
    key_count = draw_key_count(jax.random.fold_in(streams_of[7], 71), 0)
    return dict(query_rows=query_rows, key_rows=key_rows, value_rows=value_rows, grad_out=grad_out, dest_rows=dest_rows, key_blocks=key_blocks, key_count=key_count)


def attend(query_block, grad_block, key_all, value_all, block_list, list_count, block_index):
    span = KL * BLK
    groups = QH // KVH
    scaling = 1.0 / (HD ** 0.5)
    key_sel = key_all[block_list].reshape(span, KVH, HD).astype(jnp.float32)
    value_sel = value_all[block_list].reshape(span, KVH, HD).astype(jnp.float32)
    query_heads = query_block.reshape(BLK, KVH, groups, HD).astype(jnp.float32)
    grad_heads = grad_block.reshape(BLK, KVH, groups, HD).astype(jnp.float32)
    slot_index = jnp.arange(span, dtype=jnp.int32) // BLK
    is_valid = slot_index < list_count
    is_own = block_list[slot_index] == block_index
    query_pos = jnp.arange(BLK, dtype=jnp.int32)[:, None]
    key_pos = (jnp.arange(span, dtype=jnp.int32) % BLK)[None, :]
    allowed = is_valid[None, :] & (jnp.logical_not(is_own)[None, :] | (query_pos >= key_pos))
    scores = jnp.einsum("qhgd,khd->hgqk", query_heads, key_sel) * scaling
    scores = jnp.where(allowed, scores, -jnp.inf)
    row_max = jnp.max(scores, axis=-1, keepdims=True)
    weights = jnp.exp(scores - row_max)
    probability = weights / jnp.sum(weights, axis=-1, keepdims=True)
    prob_low = probability.astype(jnp.bfloat16).astype(jnp.float32)
    output = jnp.einsum("hgqk,khd->qhgd", prob_low, value_sel).astype(jnp.bfloat16)
    row_delta = jnp.sum(grad_heads * output.astype(jnp.float32), axis=-1)
    row_delta = jnp.transpose(row_delta, (1, 2, 0))[..., None]
    grad_probs = jnp.einsum("qhgd,khd->hgqk", grad_heads, value_sel)
    grad_scores = (probability * (grad_probs - row_delta)).astype(jnp.bfloat16).astype(jnp.float32)
    grad_query = (jnp.einsum("hgqk,khd->qhgd", grad_scores, key_sel) * scaling).astype(jnp.bfloat16)
    grad_key = jnp.einsum("hgqk,qhgd->khd", grad_scores, query_heads) * scaling
    grad_value = jnp.einsum("hgqk,qhgd->khd", prob_low, grad_heads)
    return (output.reshape(BLK, QH * HD), grad_query.reshape(BLK, QH * HD),
            grad_key.reshape(KL, BLK, KVH * HD), grad_value.reshape(KL, BLK, KVH * HD))


def group_pass(inputs):
    query_seq, key_seq, value_seq, grad_seq, block_lists, list_counts = inputs
    key_all = key_seq.reshape(NB, BLK, KVH * HD)
    value_all = value_seq.reshape(NB, BLK, KVH * HD)

    def one_block(block_inputs):
        query_block, grad_block, block_list, list_count, block_index = block_inputs
        return attend(query_block, grad_block, key_all, value_all, block_list, list_count, block_index)

    output, grad_query, key_parts, value_parts = lax.map(one_block, (
        query_seq.reshape(NB, BLK, QH * HD), grad_seq.reshape(NB, BLK, QH * HD),
        block_lists, list_counts, jnp.arange(NB, dtype=jnp.int32)))
    grad_key = jnp.zeros((NB, BLK, KVH * HD), jnp.float32).at[block_lists].add(key_parts)
    grad_value = jnp.zeros((NB, BLK, KVH * HD), jnp.float32).at[block_lists].add(value_parts)
    return (output.reshape(SEQ, QH * HD), grad_query.reshape(SEQ, QH * HD),
            grad_key.reshape(SEQ, KVH * HD).astype(jnp.bfloat16),
            grad_value.reshape(SEQ, KVH * HD).astype(jnp.bfloat16))


def reference(query_rows, key_rows, value_rows, grad_out, dest_rows, key_blocks, key_count):
    query_learn = jnp.zeros_like(query_rows).at[dest_rows].set(query_rows)
    key_learn = jnp.zeros_like(key_rows).at[dest_rows].set(key_rows)
    value_learn = jnp.zeros_like(value_rows).at[dest_rows].set(value_rows)
    grad_learn = jnp.zeros_like(grad_out).at[dest_rows].set(grad_out)
    groups_count = TOKENS // SEQ
    output, grad_query, grad_key, grad_value = lax.map(group_pass, (
        query_learn.reshape(groups_count, SEQ, QH * HD),
        key_learn.reshape(groups_count, SEQ, KVH * HD),
        value_learn.reshape(groups_count, SEQ, KVH * HD),
        grad_learn.reshape(groups_count, SEQ, QH * HD),
        key_blocks, key_count))
    return (output.reshape(TOKENS, QH * HD), grad_query.reshape(TOKENS, QH * HD),
            grad_key.reshape(TOKENS, KVH * HD), grad_value.reshape(TOKENS, KVH * HD))
```

```python
import functools

import jax
import jax.numpy as jnp
from jax import lax
from jax.experimental import pallas as pl
from jax.experimental.pallas import tpu as pltpu
from jax.sharding import PartitionSpec as P

QH = 64
KVH = 8
HD = 128
BLK = 128
HALF = KVH // 2
GRP = QH // KVH
SLOTS = 7
SCALE = 1.0 / HD**0.5
LOG2E = 1.4426950408889634
CHUNKS = ((0, 2), (2, 2))
UNIT = 768
VMEM_LIMIT = 56 * 1024 * 1024
INTERPRET = False
F32 = jnp.float32
BF16 = jnp.bfloat16
NT = (((1,), (1,)), ((), ()))


def dot(a, b):
    return jnp.dot(a, b, preferred_element_type=F32)


def dot_nt(a, b):
    return lax.dot_general(a, b, NT, preferred_element_type=F32)


def params():
    return pltpu.CompilerParams(vmem_limit_bytes=VMEM_LIMIT)


def one_hot(mask):
    return jnp.where(mask, 1.0, 0.0).astype(BF16)


def send_kernel(heads, with_pos, dcol, drow, q_ref, g_ref, k_ref, v_ref, out_ref, m1, m2):
    core, head = pl.program_id(0), pl.program_id(1)

    @pl.when((core == 0) & (head == 0))
    def _():
        less = jnp.where(dcol[...] < drow[...], 1.0, 0.0)
        rank = jnp.sum(less, axis=0, keepdims=True).astype(jnp.int32)
        row = lax.broadcasted_iota(jnp.int32, (1024, 256), 0)
        want = 4 * (row >> 4) + (row & 3)
        for part in range(4):
            wanted = jnp.where(((row >> 2) & 3) == part, want, -1)
            m1[:, part * 256 : part * 256 + 256] = one_hot(wanted == rank)
        m2[...] = one_hot((16 * (row >> 6) + (row & 15)) == rank)

    kv = jnp.concatenate([k_ref[...], v_ref[...]], axis=1)

    @pl.loop(0, 4)
    def _(step):
        rows = pl.ds(pl.multiple_of(step * 256, 256), 256)
        tiles = pl.ds(step * 16, 16)
        lanes = pl.multiple_of(head * UNIT, 128)
        acc = dot(m1[rows, 0:256], q_ref[:, 0:512])
        acc += dot(m1[rows, 256:512], q_ref[:, 512:1024])
        acc += dot(m1[rows, 512:768], g_ref[:, 0:512])
        acc += dot(m1[rows, 768:1024], g_ref[:, 512:1024])
        out_ref[tiles, 0, :, pl.ds(lanes, 512)] = acc.astype(BF16).reshape(16, 16, 512)
        out_ref[tiles, 0, :, pl.ds(lanes + 512, 256)] = (
            dot(m2[rows, :], kv).astype(BF16).reshape(16, 16, 256)
        )
        if with_pos:
            pos = dcol[...] & 2047
            lane = lax.broadcasted_iota(jnp.int32, (256, 128), 1)
            feature = jnp.where((lane & 32) == 0, pos >> 7, pos & 127).astype(F32).astype(BF16)
            any_part = (
                m1[rows, 0:256] + m1[rows, 256:512] + m1[rows, 512:768] + m1[rows, 768:1024]
            )
            of_kv = dot(m2[rows, :], feature)
            of_q = dot(any_part, feature)
            lane = lax.broadcasted_iota(jnp.int32, (256, 128), 1)
            out_ref[tiles, 0, :, heads * UNIT : heads * UNIT + 128] = (
                jnp.where(lane < 64, of_kv, of_q).astype(BF16).reshape(16, 16, 128)
            )


def send(first, heads, with_pos, dest, query, key, value, grad):
    width = heads * UNIT + (128 if with_pos else 0)
    wide = pl.BlockSpec((256, 1024), lambda c, h: (0, HALF * c + first + h))
    thin = pl.BlockSpec((256, 128), lambda c, h: (0, HALF * c + first + h))
    out = pl.pallas_call(
        functools.partial(send_kernel, heads, with_pos),
        grid=(2, heads),
        in_specs=[
            pl.BlockSpec((256, 1), lambda c, h: (0, 0)),
            pl.BlockSpec((1, 256), lambda c, h: (0, 0)),
            wide,
            wide,
            thin,
            thin,
        ],
        out_specs=pl.BlockSpec((64, 1, 16, width), lambda c, h: (0, c, 0, 0)),
        out_shape=jax.ShapeDtypeStruct((64, 2, 16, width), BF16),
        scratch_shapes=[pltpu.VMEM((1024, 1024), BF16), pltpu.VMEM((1024, 256), BF16)],
        compiler_params=params(),
        cost_estimate=pl.CostEstimate(
            flops=heads * 2 * 2 * 1024 * 1024 * 640,
            bytes_accessed=heads * 2 * 4 * 1024 * 1024,
            transcendentals=0,
        ),
        interpret=INTERPRET,
        name="send",
    )(dest.reshape(256, 1), dest.reshape(1, 256), query, grad, key, value)
    return out.reshape(2048, width)


def attend_tile(span, qg, kc, vc, kct, vct, dk, dv, tile, block, store):
    keys = span * BLK
    part, pair = tile >> 1, (tile & 1) * 2
    q = qg[part, block, pl.ds(pair, 2)].reshape(256, HD)
    g = qg[part + 2, block, pl.ds(pair, 2)].reshape(256, HD)
    s = dot_nt(kc[0:keys, :], q) * (SCALE * LOG2E)
    above = lax.broadcasted_iota(jnp.int32, (BLK, 256), 0)
    below = lax.broadcasted_iota(jnp.int32, (BLK, 256), 1) & (BLK - 1)
    own = jnp.where(above <= below, s[keys - BLK :, :], -1e30)
    s = own if span == 1 else jnp.concatenate([s[: keys - BLK, :], own], axis=0)
    e = jnp.exp2(s - jnp.max(s, axis=0, keepdims=True))
    p = e * (1.0 / jnp.sum(e, axis=0, keepdims=True))
    pb = p.astype(BF16)
    out = jnp.transpose(dot(vct[:, 0:keys], pb))
    t = p * dot_nt(vc[0:keys, :], g)
    delta = jnp.sum(t, axis=0, keepdims=True)
    ds = (t - p * delta).astype(BF16)
    dq = jnp.transpose(dot(kct[:, 0:keys], ds)) * SCALE
    dk[0:keys, :] += dot(ds, q)
    dv[0:keys, :] += dot(pb, g)
    store(out.astype(BF16), dq.astype(BF16))


def attend_kernel(
    aliased, sc, recv, pos_ref, *rest
):
    rest = rest[2:] if aliased else rest
    ao, dqo, theirs, own, msg1, msg2, msg3 = rest[:7]
    mq, mkv, qg, ks, vs, kts, vts, kc, vc, kct, vct, dk, dv, dks, dvs = rest[7:]
    core, chip = sc[0], sc[1]

    @pl.when(pl.program_id(0) == 0)
    def _():
        lane = lax.broadcasted_iota(jnp.int32, (16, 128), 1)
        row = lax.broadcasted_iota(jnp.int32, (16, 128), 0)
        high = jnp.where((row == 0) & (lane == 0) | (row == 1) & (lane == 64), 128.0, 0.0)
        low = jnp.where((row == 0) & (lane == 32) | (row == 1) & (lane == 96), 1.0, 0.0)
        pos = dot_nt((high + low).astype(BF16), pos_ref[...]).astype(jnp.int32)
        pos_kv = pos[0:1, :]
        pos_q = pos[1:2, :] - 512 * chip
        pos_q = ((((pos_q >> 7) + 2 * core + 2) & 3) << 7) + (pos_q & 127)
        for slot in range(SLOTS):
            if slot < 3:
                block = sc[2 + slot]
            else:
                block = 4 * chip + ((slot - 3 + 2 - 2 * core) & 3)
            inner = lax.broadcasted_iota(jnp.int32, (BLK, 2048), 0)
            mkv[slot * BLK : slot * BLK + BLK, :] = one_hot(inner == pos_kv - block * BLK)
        part_of = (lax.broadcasted_iota(jnp.int32, (1, 2048), 1) >> 2) & 3
        for part in range(4):
            pos_part = jnp.where(part_of == part, pos_q, -1)
            for block in range(4):
                inner = lax.broadcasted_iota(jnp.int32, (BLK, 2048), 0)
                mq[part, block * BLK : block * BLK + BLK, :] = one_hot(
                    inner == pos_part - block * BLK
                )

    @pl.loop(0, 4)
    def _(part):
        placed = dot(mq[part], recv[:, 0:512]).astype(BF16)
        for block in range(4):
            for head in range(4):
                qg[part, block, head] = placed[
                    block * BLK : block * BLK + BLK, head * HD : head * HD + HD
                ]

    @pl.loop(0, SLOTS)
    def _(slot):
        rows = pl.ds(pl.multiple_of(slot * BLK, BLK), BLK)
        kv = dot(mkv[rows, :], recv[:, 512:768])
        ks[slot] = kv[:, 0:HD].astype(BF16)
        vs[slot] = kv[:, HD : 2 * HD].astype(BF16)
        kts[slot] = jnp.transpose(kv[:, 0:HD]).astype(BF16)
        vts[slot] = jnp.transpose(kv[:, HD : 2 * HD]).astype(BF16)

    dks[...] = jnp.zeros_like(dks)
    dvs[...] = jnp.zeros_like(dvs)

    @pl.loop(0, 4)
    def _(block):
        count = sc[5 + block]
        for entry in range(4):
            slot = sc[9 + 4 * block + entry]
            span = slice(entry * BLK, entry * BLK + BLK)
            kc[span, :] = ks[slot]
            vc[span, :] = vs[slot]
            kct[:, span] = kts[slot]
            vct[:, span] = vts[slot]
        dk[...] = jnp.zeros_like(dk)
        dv[...] = jnp.zeros_like(dv)

        @pl.loop(0, 4)
        def _(tile):
            def store(out, dq):
                for half in range(2):
                    lanes = pl.ds(pl.multiple_of((2 * tile + half) * HD, HD), HD)
                    piece = slice(half * BLK, half * BLK + BLK)

                    @pl.when(block < 2)
                    def _():
                        rows = pl.ds(pl.multiple_of(block * BLK, BLK), BLK)
                        theirs[0, rows, lanes] = out[piece, :]
                        theirs[1, rows, lanes] = dq[piece, :]

                    @pl.when(block >= 2)
                    def _():
                        rows = pl.ds(pl.multiple_of((block - 2) * BLK, BLK), BLK)
                        ao[rows, lanes] = out[piece, :]
                        dqo[rows, lanes] = dq[piece, :]

            for span in range(1, 5):

                @pl.when(count == span)
                def _():
                    attend_tile(
                        span, qg, kc, vc, kct, vct, dk, dv, tile, block, store
                    )

        for entry in range(4):
            slot = sc[9 + 4 * block + entry]
            span = slice(entry * BLK, entry * BLK + BLK)

            @pl.when(entry < count)
            def _():
                dks[slot] += dk[span, :]
                dvs[slot] += dv[span, :]

    for rel in range(4):
        own[rel * BLK : rel * BLK + BLK, 0:HD] = dks[3 + rel] * SCALE
        own[rel * BLK : rel * BLK + BLK, HD : 2 * HD] = dvs[3 + rel]
    for dist, msg in ((1, msg1), (2, msg2), (3, msg3)):
        size = msg.shape[0] - 16
        msg[...] = jnp.zeros_like(msg)
        row = lax.broadcasted_iota(jnp.int32, (16, 2 * HD), 0)
        head = jnp.full((16, 2 * HD), 9.0, F32)
        for slot in range(3):
            hit = sc[25 + slot] == dist
            place = sc[28 + slot]
            name = ((sc[2 + slot] + 2 * core + 2) & 3).astype(F32)
            head = jnp.where((row == place) & hit, name, head)

            @pl.when(hit)
            def _():
                rows = pl.ds(pl.multiple_of(place * BLK, BLK), BLK)
                msg[rows, 0:HD] = (dks[slot] * SCALE).astype(BF16)
                msg[rows, HD : 2 * HD] = dvs[slot].astype(BF16)

        msg[size:, :] = head.astype(BF16)


def attend(first, heads, scalars, recv, pos, pos_at, ao, dqo):
    aliased = ao is not None
    full = jax.ShapeDtypeStruct((256, QH * HD), BF16)
    mine = pl.BlockSpec((256, 1024), lambda h, sc: (0, HALF * sc[0] + first + h))
    column = lambda rows: pl.BlockSpec((rows, 2 * HD), lambda h, sc: (0, h))
    unit = UNIT
    specs = [
        pl.BlockSpec((2048, unit), lambda h, sc: (0, h)),
        pl.BlockSpec((2048, 128), lambda h, sc: (0, pos_at)),
    ]
    args = [recv, pos]
    if aliased:
        specs += [pl.BlockSpec(memory_space=pl.ANY)] * 2
        args += [ao, dqo]
    lengths = (3 * BLK + 16, 2 * BLK + 16, 2 * BLK + 16)
    return pl.pallas_call(
        functools.partial(attend_kernel, aliased),
        grid_spec=pltpu.PrefetchScalarGridSpec(
            num_scalar_prefetch=1,
            grid=(heads,),
            in_specs=specs,
            out_specs=[
                mine,
                mine,
                pl.BlockSpec((2, 256, 1024), lambda h, sc: (0, 0, h)),
                column(512),
            ]
            + [column(length) for length in lengths],
            scratch_shapes=[
                pltpu.VMEM((4, 512, 2048), BF16),
                pltpu.VMEM((SLOTS * BLK, 2048), BF16),
                pltpu.VMEM((4, 4, 4, BLK, HD), BF16),
            ]
            + [pltpu.VMEM((SLOTS, BLK, HD), BF16)] * 4
            + [pltpu.VMEM((4 * BLK, HD), BF16)] * 2
            + [pltpu.VMEM((HD, 4 * BLK), BF16)] * 2
            + [pltpu.VMEM((4 * BLK, HD), F32)] * 2
            + [pltpu.VMEM((SLOTS, BLK, HD), F32)] * 2,
        ),
        out_shape=[
            full,
            full,
            jax.ShapeDtypeStruct((2, 256, heads * 1024), BF16),
            jax.ShapeDtypeStruct((512, heads * 2 * HD), F32),
        ]
        + [jax.ShapeDtypeStruct((length, heads * 2 * HD), BF16) for length in lengths],
        input_output_aliases={3: 0, 4: 1} if aliased else {},
        compiler_params=params(),
        cost_estimate=pl.CostEstimate(
            flops=heads * 16 * 1024**3,
            bytes_accessed=heads * 9 * 1024 * 1024,
            transcendentals=heads * 512 * 8 * 512,
        ),
        interpret=INTERPRET,
        name="attend",
    )(scalars, *args)


def sum_kernel(own, msg1, msg2, msg3, mine, theirs):
    total = [own[rel * BLK : rel * BLK + BLK, :] for rel in range(4)]
    for msg in (msg1, msg2, msg3):
        size = msg.shape[0] - 16
        head = msg[size:, :].astype(F32)
        for slot in range(size // BLK):
            name = head[slot : slot + 1, :]
            value = msg[slot * BLK : slot * BLK + BLK, :].astype(F32)
            for rel in range(4):
                total[rel] = total[rel] + jnp.where(name == float(rel), value, 0.0)
    for half in range(2):
        theirs[half * BLK : half * BLK + BLK, :] = total[half].astype(BF16)
        mine[half * BLK : half * BLK + BLK, :] = total[2 + half].astype(BF16)


def sum_grads(heads, own, msgs):
    column = lambda rows: pl.BlockSpec((rows, 2 * HD), lambda h: (0, h))
    shape = jax.ShapeDtypeStruct((256, heads * 2 * HD), BF16)
    return pl.pallas_call(
        sum_kernel,
        grid=(heads,),
        in_specs=[column(512)] + [column(msg.shape[0]) for msg in msgs],
        out_specs=[column(256)] * 2,
        out_shape=[shape] * 2,
        compiler_params=params(),
        interpret=INTERPRET,
        name="sum_grads",
    )(own, *msgs)


def place_kernel(sc, got_out, got_dq, ao_in, dqo_in, ao, dqo):
    ao[...] = got_out[0]
    dqo[...] = got_dq[0]


def place(first, heads, scalars, got, ao, dqo):
    out = pl.BlockSpec((256, 1024), lambda h, sc: (0, HALF * (1 - sc[0]) + first + h))
    full = jax.ShapeDtypeStruct((256, QH * HD), BF16)
    return pl.pallas_call(
        place_kernel,
        grid_spec=pltpu.PrefetchScalarGridSpec(
            num_scalar_prefetch=1,
            grid=(heads,),
            in_specs=[
                pl.BlockSpec((1, 256, 1024), lambda h, sc: (0, 0, h)),
                pl.BlockSpec((1, 256, 1024), lambda h, sc: (1, 0, h)),
                pl.BlockSpec(memory_space=pl.ANY),
                pl.BlockSpec(memory_space=pl.ANY),
            ],
            out_specs=[out, out],
        ),
        out_shape=[full, full],
        input_output_aliases={3: 0, 4: 1},
        compiler_params=params(),
        cost_estimate=pl.CostEstimate(
            flops=0, bytes_accessed=heads * 2 * 1024 * 1024, transcendentals=0
        ),
        interpret=INTERPRET,
        name="place",
    )(scalars, got, got, ao, dqo)


def gather_kernel(chunks, sc, *refs):
    dk, dv = refs[-2:]
    for index, (first, heads) in enumerate(chunks):
        for which in range(2):
            piece = refs[2 * index + which]
            core = sc[0] if which == 0 else 1 - sc[0]
            for head in range(heads):
                lanes = pl.ds(pl.multiple_of((HALF * core + first + head) * HD, HD), HD)
                dk[:, lanes] = piece[:, head * 256 : head * 256 + 128]
                dv[:, lanes] = piece[:, head * 256 + 128 : head * 256 + 256]


def gather_grads(scalars, pieces):
    whole = lambda width: pl.BlockSpec((256, width), lambda i, sc: (0, 0))
    shape = jax.ShapeDtypeStruct((256, KVH * HD), BF16)
    return pl.pallas_call(
        functools.partial(gather_kernel, CHUNKS),
        grid_spec=pltpu.PrefetchScalarGridSpec(
            num_scalar_prefetch=1,
            grid=(1,),
            in_specs=[whole(piece.shape[1]) for piece in pieces],
            out_specs=[whole(KVH * HD)] * 2,
        ),
        out_shape=[shape, shape],
        compiler_params=params(),
        interpret=INTERPRET,
        name="gather_grads",
    )(scalars, *pieces)


def plan(chip, core, lists, counts):
    numbers = jnp.arange(16, dtype=jnp.int32)
    valid = jnp.arange(4, dtype=jnp.int32)[None, :] < counts[:, None]
    listed = (lists.reshape(16, 1) == numbers[None, :]) & valid.reshape(16, 1)
    remote = jnp.any(listed, axis=0) & (numbers < 4 * chip)
    remote_int = remote.astype(jnp.int32)
    rank = jnp.sum(
        jnp.where(numbers[:, None] < numbers[None, :], remote_int[:, None], 0), axis=0
    )
    three = jnp.arange(3, dtype=jnp.int32)
    chosen = remote[None, :] & (rank[None, :] == three[:, None])
    blocks = jnp.sum(jnp.where(chosen, numbers[None, :] + 1, 0), axis=1) - 1
    local = 3 + ((lists - 4 * chip + 2 * core + 2) & 3)
    far = jnp.sum(jnp.where(lists[:, :, None] == numbers, rank, 0), axis=-1)
    slots = jnp.where(lists >= 4 * chip, local, jnp.minimum(far, 2))
    dist = jnp.where(blocks >= 0, chip - (blocks >> 2), 0)
    place_of = jnp.sum(
        jnp.where(
            (dist[None, :] == dist[:, None]) & (three[None, :] < three[:, None]), 1, 0
        ),
        axis=1,
    )
    return jnp.concatenate(
        [jnp.stack([core, chip]), blocks, counts, slots.reshape(16), dist, place_of]
    ).astype(jnp.int32)


def body(query_rows, key_rows, value_rows, grad_out, dest_rows, key_blocks, key_count):
    own_index = lax.axis_index("ctx")
    chip, core = own_index >> 1, own_index & 1
    swap = [(i, i ^ 1) for i in range(8)]
    back = lambda dist: [(i, i - 2 * dist) for i in range(2 * dist, 8)]

    sent = []
    for index, (first, heads) in enumerate(CHUNKS):
        sent.append(
            send(first, heads, index == 0, dest_rows, query_rows, key_rows, value_rows, grad_out)
        )
    got = [lax.all_to_all(x, ("dp", "ctx"), 0, 0, tiled=True) for x in sent]

    table = jnp.concatenate([key_blocks[0], key_count[0][:, None]], axis=1)
    table = jnp.concatenate([lax.ppermute(table, "ctx", swap), table], axis=0)
    scalars = plan(chip, core, table[:, :4], table[:, 4])

    ao = dqo = None
    pieces = []
    for index, (first, heads) in enumerate(CHUNKS):
        ao, dqo, theirs, own, *msgs = attend(
            first, heads, scalars, got[index], got[0], CHUNKS[0][1] * UNIT // 128, ao, dqo
        )
        msgs = [lax.ppermute(msg, "ctx", back(dist + 1)) for dist, msg in enumerate(msgs)]
        passed = lax.ppermute(theirs, "ctx", swap)
        ao, dqo = place(first, heads, scalars, passed, ao, dqo)
        mine, others = sum_grads(heads, own, msgs)
        pieces += [mine, lax.ppermute(others, "ctx", swap)]
    dk, dv = gather_grads(scalars, pieces)
    return ao, dqo, dk, dv


def solution(mesh):
    rows = P(("dp", "ctx"), None)
    return jax.shard_map(
        body,
        mesh=mesh,
        in_specs=(
            rows,
            rows,
            rows,
            rows,
            P(("dp", "ctx")),
            P("dp", "ctx", None),
            P("dp", "ctx"),
        ),
        out_specs=(rows, rows, rows, rows),
        check_vma=False,
    )
```
